32 devices in a mesh: row: 8 (over z, core), col: 4 (over y, x).
Axes of the slice: x: 2, y: 2, z: 4, core: 2. Of those that a mesh axis runs over, the one named last changes fastest.
Arguments:
- tokens: bfloat16 [16384, 1024], P('row', 'col'), may hold values from -6 to 6
- memory: bfloat16 [4096, 1024], P('row', 'col'), may hold values from -6 to 6
- old_memory: bfloat16 [12288, 1024], P('row', 'col'), may hold values from -6 to 6
- doc_ids: int32 [8, 4096], P('row'), may hold values from 0 to 5, as said below
- norm_gains: bfloat16 [2, 1024], P(None, 'row'), may hold values from 0.5 to 1.5
- comp_weight: bfloat16 [3072, 1024], P('row', 'col'), may hold values from -0.109375 to 0.109375
- query_weight: bfloat16 [1024, 1024], P('row', 'col'), may hold values from -0.1875 to 0.1875
- key_weight: bfloat16 [1024, 1024], P('row', 'col'), may hold values from -0.1875 to 0.1875
- value_weight: bfloat16 [1024, 1024], P('row', 'col'), may hold values from -0.1875 to 0.1875
- proj_weight: bfloat16 [1024, 1024], P('col', 'row'), may hold values from -1.5 to 1.5
- up_weight: bfloat16 [1024, 4096], P('row', 'col'), may hold values from -0.1875 to 0.1875
- down_weight: bfloat16 [4096, 1024], P('col', 'row'), may hold values from -0.09375 to 0.09375
- cotangent: bfloat16 [16384, 1024], P('row', 'col'), may hold values from -6 to 6
Outputs:
- layer_out: bfloat16 [16384, 1024], P('row', 'col')
- grad_x: float32 [16384, 1024], P('row', 'col')
- grad_gains: float32 [2, 1024], P(None, 'row')
- grad_comp: float32 [3072, 1024], P('row', 'col')
- grad_query: float32 [1024, 1024], P('row', 'col')
- grad_key: float32 [1024, 1024], P('row', 'col')
- grad_value: float32 [1024, 1024], P('row', 'col')
- grad_proj: float32 [1024, 1024], P('col', 'row')
- grad_up: float32 [1024, 4096], P('row', 'col')
- grad_down: float32 [4096, 1024], P('col', 'row')
The draws below stay inside these ranges and needn't reach their ends.
Inputs may be any that keep to these rules, and one draw needn't show every extreme that they name: In each row of doc_ids the numbers never fall and every number occurs; every document covers 200 entries or more.
All inputs are finite; a program needn't handle non-finite values.
Results may differ from the reference program's by a relative error of at most 0.015.
Values may be sent and summed in bfloat16 or wider, within the bound.
A program may use at most 192 MiB of HBM per device.

```python
import jax
import jax.numpy as jnp
from jax import lax

D = 1024
HEADS = 8
FF = 4096
MEM = 512
CM = 512
RATE = 3
DOC_LEAST = 200
SEQ = 2048
HD = 128
SPAN = 4096
DOCS = 6
TOKENS = 16384
N_ROW = 8


def draw_doc_ids(key, part):
    base = SPAN // DOCS
    jitter = max(0, (base - DOC_LEAST) // 2)
    moves = jax.random.randint(key, (N_ROW, DOCS - 1), -jitter, jitter + 1)
    bounds = base * jnp.arange(1, DOCS, dtype=jnp.int32)[None, :] + moves
    places = jnp.arange(SPAN, dtype=jnp.int32)
    return jnp.sum((places[None, :, None] >= bounds[:, None, :]).astype(jnp.int32), axis=-1)


def block_scale(stream_key, extent, cuts, least, largest):
    level = 1.0
    for dim, blocks in cuts:
        steps = jax.random.uniform(jax.random.fold_in(jax.random.fold_in(stream_key, 6), dim), (blocks,), jnp.float32, least / len(cuts), largest / len(cuts))
        level = level * jnp.repeat(jnp.exp(steps), extent[dim] // blocks).reshape((-1,) + (1,) * (len(extent) - 1 - dim))
    return level


def noise(own_key, dims, scale, bound, pieces=(), held_as=jnp.bfloat16):
    loudness = block_scale(own_key, dims, pieces, -0.22, 0.18) if pieces else 1.0
    array = jax.random.normal(own_key, dims, jnp.float32) * scale * loudness
    return jnp.minimum(jnp.maximum(array, -bound), bound).astype(held_as)


def setup_inputs(seed: int = 0) -> dict:
    key_of = jax.random.split(jax.random.key(seed), 14)
    return {
        "tokens": noise(key_of[0], (TOKENS, D), 1.0, 6.0, ((0, 8), (1, 4))),
        "memory": noise(key_of[1], (N_ROW * MEM, D), 1.0, 6.0, ((0, 8), (1, 4))),
        "old_memory": noise(key_of[2], (N_ROW * RATE * CM, D), 1.0, 6.0, ((0, 8), (1, 4))),
        "doc_ids": draw_doc_ids(jax.random.fold_in(key_of[13], 71), 0),
        "norm_gains": jnp.clip(1.0 + 0.1 * jax.random.normal(key_of[4], (2, D), jnp.float32), 0.5, 1.5).astype(jnp.bfloat16),
        "comp_weight": noise(key_of[5], (RATE * D, D), (RATE * D) ** -0.5, 0.109375, ((0, 8), (1, 4))),
        "query_weight": noise(key_of[6], (D, D), D ** -0.5, 0.1875, ((0, 8), (1, 4))),
        "key_weight": noise(key_of[7], (D, D), D ** -0.5, 0.1875, ((0, 8), (1, 4))),
        "value_weight": noise(key_of[8], (D, D), D ** -0.5, 0.1875, ((0, 8), (1, 4))),
        "proj_weight": noise(key_of[9], (D, D), (max(1, D // 64)) ** -0.5, 1.5, ((0, 4), (1, 8))),
        "up_weight": noise(key_of[10], (D, FF), D ** -0.5, 0.1875, ((0, 8), (1, 4))),
        "down_weight": noise(key_of[11], (FF, D), FF ** -0.5, 0.09375, ((0, 4), (1, 8))),
        "cotangent": noise(key_of[12], (TOKENS, D), 1.0, 6.0, ((0, 8), (1, 4))),
    }


@jax.custom_vjp
def low(v):
    return lax.optimization_barrier(v.astype(jnp.bfloat16)).astype(jnp.float32)

@jax.custom_vjp
def low_back(v):
    return v

def low_keep(v):
    return (low(v), None)

def low_pass(kept, grad):
    return (grad,)

def back_keep(v):
    return (v, None)

def back_low(kept, grad):
    return (low(grad),)
low.defvjp(low_keep, low_pass)
low_back.defvjp(back_keep, back_low)

def matmul(left, right):
    return jnp.dot(left, right, precision=lax.Precision.HIGHEST)

def normalize(rows, gain):
    centre = rows - lax.optimization_barrier(jnp.mean(rows, axis=-1, keepdims=True))
    spread = lax.optimization_barrier(jnp.mean(centre * centre, axis=-1, keepdims=True))
    return centre * lax.rsqrt(spread + 1e-05) * gain

def layer(params, token_rows, memory_rows, old_rows, doc_row):
    gains, comp_w, query_w, key_w, value_w, proj_w, up_w, down_w = params
    compressed = low_back(low(matmul(old_rows.reshape(CM, RATE * D), comp_w)))
    stacked = jnp.concatenate([compressed, memory_rows, token_rows], axis=0)
    normed = low(normalize(stacked, gains[0]))
    queries = low_back(low(matmul(normed[CM + MEM:], query_w)))
    keys = low_back(low(matmul(normed, key_w)))
    values = low_back(low(matmul(normed, value_w)))
    key_doc = jnp.concatenate([doc_row[RATE - 1:RATE * CM:RATE], doc_row[RATE * CM:]])
    key_place = jnp.arange(CM + MEM + SEQ, dtype=jnp.int32) - (CM + MEM)
    query_doc = doc_row[RATE * CM + MEM:]
    query_place = jnp.arange(SEQ, dtype=jnp.int32)
    block = min(512, SEQ)
    steps_count = SEQ // block
    scale = HD ** (-0.5)
    key_heads = keys.reshape(CM + MEM + SEQ, HEADS, HD)
    value_heads = values.reshape(CM + MEM + SEQ, HEADS, HD)

    def one_block(items):
        query_block, doc_block, place_block = items
        allowed = (doc_block[:, None] == key_doc[None, :]) & (key_place[None, :] <= place_block[:, None])
        scores = jnp.einsum('qhd,khd->hqk', query_block, key_heads, precision=lax.Precision.HIGHEST) * scale
        scores = low_back(scores)
        scores = jnp.where(allowed[None], scores, -1e+30)
        weights = low(jax.nn.softmax(scores, axis=-1))
        return jnp.einsum('hqk,khd->qhd', weights, value_heads, precision=lax.Precision.HIGHEST)
    mixed = lax.map(jax.checkpoint(one_block), (queries.reshape(steps_count, block, HEADS, HD), query_doc.reshape(steps_count, block), query_place.reshape(steps_count, block)))
    mixed = low_back(low(mixed.reshape(SEQ, D)))
    resid = token_rows + low_back(matmul(mixed, proj_w))
    hidden_in = low(normalize(resid, gains[1]))
    upper = low_back(matmul(hidden_in, up_w))
    active = low(jax.nn.gelu(upper))
    return resid + low_back(matmul(active, down_w))

def reference(tokens, memory, old_memory, doc_ids, norm_gains, comp_weight, query_weight, key_weight, value_weight, proj_weight, up_weight, down_weight, cotangent):
    params = tuple((a.astype(jnp.float32) for a in (norm_gains, comp_weight, query_weight, key_weight, value_weight, proj_weight, up_weight, down_weight)))
    groups = tokens.shape[0] // SEQ
    token_seq = tokens.astype(jnp.float32).reshape(groups, SEQ, D)
    memory_seq = memory.astype(jnp.float32).reshape(groups, MEM, D)
    old_seq = old_memory.astype(jnp.float32).reshape(groups, RATE * CM, D)
    cot_seq = cotangent.astype(jnp.float32).reshape(groups, SEQ, D)

    def step(totals, items):
        token_rows, memory_rows, old_rows, doc_row, cot_rows = items

        def forward(inputs, weights):
            return layer(weights, inputs, memory_rows, old_rows, doc_row)
        result, pull = jax.vjp(forward, token_rows, params)
        grad_in, grad_w = pull(cot_rows)
        totals = jax.tree.map(lambda a, b: a + b, totals, grad_w)
        return (totals, (result.astype(jnp.bfloat16), grad_in))
    zeros = jax.tree.map(jnp.zeros_like, params)
    totals, (outputs, grads) = lax.scan(step, zeros, (token_seq, memory_seq, old_seq, doc_ids, cot_seq))
    return (outputs.reshape(groups * SEQ, D), grads.reshape(groups * SEQ, D), totals[0], totals[1], totals[2], totals[3], totals[4], totals[5], totals[6], totals[7])
```

```python
import functools

import jax
import jax.numpy as jnp
from jax import lax
from jax.experimental import pallas as pl
from jax.experimental.pallas import tpu as pltpu
from jax.sharding import PartitionSpec as P

RATE = 3
HD = 128
EPS = 1e-05
BF = jnp.bfloat16
F32 = jnp.float32
LOG2E = 1.4426950408889634


def mm(left, right, dims, out=BF):
    return lax.dot_general(left, right, (dims, ((), ())), preferred_element_type=F32).astype(out)


def nn(left, right, out=BF):
    return mm(left, right, ((1,), (0,)), out)


def nt(left, right, out=BF):
    return mm(left, right, ((1,), (1,)), out)


def tn(left, right, out=BF):
    return mm(left, right, ((0,), (0,)), out)


def assemble_body(count, width, taps, normed, has_base, me_ref, *refs):
    me = me_ref[0]
    parts = refs[:count]
    out_ref = refs[-1]
    if not normed:
        for m in range(count):
            for t in range(taps):
                at = pl.multiple_of(t * count * width + (me ^ m) * width, width)
                out_ref[:, pl.ds(at, width)] = parts[m][:, t * width : (t + 1) * width]
        return
    gain_ref = refs[count]
    wide = count * width
    values = [part[...].astype(F32) for part in parts]
    mean = sum(jnp.sum(v, axis=-1, keepdims=True) for v in values) / wide
    centred = [v - mean for v in values]
    spread = sum(jnp.sum(c * c, axis=-1, keepdims=True) for c in centred) / wide
    inverse = lax.rsqrt(spread + EPS)
    for m in range(count):
        at = pl.multiple_of((me ^ m) * width, width)
        out_ref[:, pl.ds(at, width)] = (centred[m] * inverse * gain_ref[:, pl.ds(at, width)]).astype(BF)


def assemble(parts, me, tile, steps, source, target, out_rows, taps=1, gain=None, base=None):
    count = len(parts)
    width = parts[0].shape[1] // taps
    wide = count * width * taps
    in_specs = [
        pl.BlockSpec((tile, width * taps), lambda i, s: (source(i, s[0]), 0)) for _ in range(count)
    ]
    operands = list(parts)
    aliases = {}
    if gain is not None:
        in_specs.append(pl.BlockSpec((1, wide), lambda i, s: (0, 0)))
        operands.append(gain.reshape(1, wide))
    if base is not None:
        in_specs.append(pl.BlockSpec(memory_space=pl.ANY))
        aliases = {1 + len(operands): 0}
        operands.append(base)
    return pl.pallas_call(
        functools.partial(assemble_body, count, width, taps, gain is not None, base is not None),
        out_shape=jax.ShapeDtypeStruct((out_rows, wide), BF),
        grid_spec=pltpu.PrefetchScalarGridSpec(
            num_scalar_prefetch=1,
            grid=(steps,),
            in_specs=in_specs,
            out_specs=pl.BlockSpec((tile, wide), lambda i, s: (target(i), 0)),
        ),
        input_output_aliases=aliases,
        cost_estimate=pl.CostEstimate(
            flops=10 * steps * tile * wide, bytes_accessed=4 * steps * tile * wide, transcendentals=0
        ),
    )(me.reshape(1), *operands)


def stack_body(count, me_ref, *refs):
    me = me_ref[0]
    out_ref = refs[-1]
    high = refs[0].shape[0]
    for m in range(count):
        at = pl.multiple_of((me ^ m) * high, high)
        out_ref[pl.ds(at, high), :] = refs[m][...].astype(out_ref.dtype)


def stack_rows(parts, me, out=BF):
    count = len(parts)
    high, wide = parts[0].shape
    tile = min(wide, 256)
    return pl.pallas_call(
        functools.partial(stack_body, count),
        out_shape=jax.ShapeDtypeStruct((count * high, wide), out),
        grid_spec=pltpu.PrefetchScalarGridSpec(
            num_scalar_prefetch=1,
            grid=(wide // tile,),
            in_specs=[pl.BlockSpec((high, tile), lambda i, s: (0, i)) for _ in range(count)],
            out_specs=pl.BlockSpec((count * high, tile), lambda i, s: (0, i)),
        ),
        cost_estimate=pl.CostEstimate(
            flops=0, bytes_accessed=4 * count * high * wide, transcendentals=0
        ),
    )(me.reshape(1), *parts)


def attend_body(heads, keys_n, scale, live_ref, rows_ref, places_ref, q_ref, k_ref, v_ref, out_ref, level_ref, top_ref, total_ref, sum_ref):
    step = pl.program_id(0)
    tile = q_ref.shape[0]
    top_ref[...] = jnp.full(top_ref.shape, -1e30, F32)
    total_ref[...] = jnp.zeros(total_ref.shape, F32)
    sum_ref[...] = jnp.zeros(sum_ref.shape, F32)
    first, last = rows_ref[0:1, :], rows_ref[1:2, :]

    @pl.loop(0, keys_n)
    def _(j):
        @pl.when(live_ref[step * keys_n + j] != 0)
        def _():
            at = pl.ds(pl.multiple_of(j * tile, tile), tile)
            place = places_ref[at, 0:1]
            allowed = (place >= first) & (place <= last)
            for h in range(heads):
                cols = slice(h * HD, (h + 1) * HD)
                scores = mm(k_ref[at, cols], q_ref[:, cols], ((1,), (1,)), F32)
                scores = jnp.where(allowed, scores, -1e30)
                before = top_ref[h : h + 1, :]
                top = jnp.maximum(before, jnp.max(scores, axis=0, keepdims=True))
                raw = jnp.exp2((scores - top) * scale)
                shrink = jnp.exp2((before - top) * scale)
                top_ref[h : h + 1, :] = top
                total_ref[h : h + 1, :] = total_ref[h : h + 1, :] * shrink + jnp.sum(raw, axis=0, keepdims=True)
                sum_ref[cols, :] = sum_ref[cols, :] * shrink + mm(v_ref[at, cols], raw.astype(BF), ((0,), (0,)), F32)

    for h in range(heads):
        cols = slice(h * HD, (h + 1) * HD)
        total = total_ref[h : h + 1, :]
        out_ref[:, cols] = (sum_ref[cols, :] / total).T.astype(BF)
        level_ref[h : h + 1, :] = top_ref[h : h + 1, :] * scale + jnp.log2(total)


def attend(qkv, live, rows, places, slab, tile, per, q_tiles, first_tile):
    heads = slab // HD
    keys = qkv.shape[0]
    keys_n = keys // tile
    group = per + 1

    def row_tile(i):
        i = i + first_tile
        return (i // per) * group + 1 + i % per

    return pl.pallas_call(
        functools.partial(attend_body, heads, keys_n, LOG2E * HD ** (-0.5)),
        out_shape=(
            jax.ShapeDtypeStruct((q_tiles * tile, slab), BF),
            jax.ShapeDtypeStruct((8, q_tiles * tile), F32),
        ),
        grid_spec=pltpu.PrefetchScalarGridSpec(
            num_scalar_prefetch=1,
            grid=(q_tiles,),
            in_specs=[
                pl.BlockSpec((2, tile), lambda i, s: (0, i + first_tile)),
                pl.BlockSpec((keys, 1), lambda i, s: (0, 0)),
                pl.BlockSpec((tile, slab), lambda i, s: (row_tile(i), 0)),
                pl.BlockSpec((keys, slab), lambda i, s: (0, 1)),
                pl.BlockSpec((keys, slab), lambda i, s: (0, 2)),
            ],
            out_specs=(
                pl.BlockSpec((tile, slab), lambda i, s: (i, 0)),
                pl.BlockSpec((8, tile), lambda i, s: (0, i)),
            ),
            scratch_shapes=[
                pltpu.VMEM((8, tile), F32),
                pltpu.VMEM((8, tile), F32),
                pltpu.VMEM((slab, tile), F32),
            ],
        ),
        cost_estimate=pl.CostEstimate(
            flops=q_tiles * tile * keys * slab, bytes_accessed=4 * keys * slab, transcendentals=q_tiles * tile * keys // 2
        ),
    )(live[first_tile * keys_n : (first_tile + q_tiles) * keys_n], rows, places, qkv, qkv, qkv)


def attend_back_body(
    heads, keys_n, per, scale, live_ref, rows_ref, level_ref, places_ref, q_ref, k_ref, v_ref, o_ref, g_ref, out_ref, dk_ref, dv_ref, dq_ref
):
    step = pl.program_id(0)
    tile, slab = q_ref.shape
    first, last = rows_ref[0:1, :], rows_ref[1:2, :]
    factor = HD ** (-0.5)

    @pl.when(step == 0)
    def _():
        dk_ref[...] = jnp.zeros(dk_ref.shape, F32)
        dv_ref[...] = jnp.zeros(dv_ref.shape, F32)

    dq_ref[...] = jnp.zeros(dq_ref.shape, F32)
    inner = (o_ref[...].astype(F32) * g_ref[...].astype(F32)).T
    deltas = [jnp.sum(inner[h * HD : (h + 1) * HD], axis=0, keepdims=True) for h in range(heads)]

    @pl.loop(0, keys_n)
    def _(j):
        @pl.when(live_ref[step * keys_n + j] != 0)
        def _():
            at = pl.ds(pl.multiple_of(j * tile, tile), tile)
            place = places_ref[at, 0:1]
            allowed = (place >= first) & (place <= last)
            for h in range(heads):
                cols = slice(h * HD, (h + 1) * HD)
                q, k, v, g = q_ref[:, cols], k_ref[at, cols], v_ref[at, cols], g_ref[:, cols]
                scores = mm(k, q, ((1,), (1,)), F32)
                probs = jnp.where(allowed, jnp.exp2(scores * scale - level_ref[h : h + 1, :]), 0.0)
                dprobs = mm(v, g, ((1,), (1,)), F32)
                dscores = (probs * (dprobs - deltas[h])).astype(BF)
                dv_ref[at, cols] += mm(probs.astype(BF), g, ((1,), (0,)), F32)
                dk_ref[at, cols] += mm(dscores, q, ((1,), (0,)), F32)
                dq_ref[cols, :] += mm(k, dscores, ((0,), (0,)), F32)

    row = (step // per) * (per + 1) + 1 + step % per
    out_ref[pl.ds(pl.multiple_of(row * tile, tile), tile), 0:slab] = (dq_ref[...].T * factor).astype(BF)

    @pl.when(step % per == 0)
    def _():
        out_ref[pl.ds(pl.multiple_of((row - 1) * tile, tile), tile), 0:slab] = jnp.zeros((tile, slab), BF)

    @pl.when(step == pl.num_programs(0) - 1)
    def _():
        @pl.loop(0, keys_n)
        def _(j):
            at = pl.ds(pl.multiple_of(j * tile, tile), tile)
            out_ref[at, slab : 2 * slab] = (dk_ref[at, :] * factor).astype(BF)
            out_ref[at, 2 * slab :] = dv_ref[at, :].astype(BF)


def attend_back(qkv, live, rows, level, places, mixed, grad, slab, tile, per):
    heads = slab // HD
    keys = qkv.shape[0]
    keys_n = keys // tile
    q_tiles = mixed.shape[0] // tile
    group = per + 1
    return pl.pallas_call(
        functools.partial(attend_back_body, heads, keys_n, per, LOG2E * HD ** (-0.5)),
        out_shape=jax.ShapeDtypeStruct((keys, 3 * slab), BF),
        grid_spec=pltpu.PrefetchScalarGridSpec(
            num_scalar_prefetch=1,
            grid=(q_tiles,),
            in_specs=[
                pl.BlockSpec((2, tile), lambda i, s: (0, i)),
                pl.BlockSpec((8, tile), lambda i, s: (0, i)),
                pl.BlockSpec((keys, 1), lambda i, s: (0, 0)),
                pl.BlockSpec((tile, slab), lambda i, s: ((i // per) * group + 1 + i % per, 0)),
                pl.BlockSpec((keys, slab), lambda i, s: (0, 1)),
                pl.BlockSpec((keys, slab), lambda i, s: (0, 2)),
                pl.BlockSpec((tile, slab), lambda i, s: (i, 0)),
                pl.BlockSpec((tile, slab), lambda i, s: (i, 0)),
            ],
            out_specs=pl.BlockSpec((keys, 3 * slab), lambda i, s: (0, 0)),
            scratch_shapes=[
                pltpu.VMEM((keys, slab), F32),
                pltpu.VMEM((keys, slab), F32),
                pltpu.VMEM((slab, tile), F32),
            ],
        ),
        cost_estimate=pl.CostEstimate(
            flops=3 * q_tiles * tile * keys * slab, bytes_accessed=12 * keys * slab, transcendentals=q_tiles * tile * keys // 2
        ),
    )(live, rows, level, places, qkv, qkv, qkv, mixed, grad)


def statistics(rows):
    centre = rows - jnp.mean(rows, axis=-1, keepdims=True)
    inverse = lax.rsqrt(jnp.mean(centre * centre, axis=-1, keepdims=True) + EPS)
    return centre * inverse, inverse


def norm_back(rows, gain, grad):
    unit, inverse = statistics(rows)
    lifted = gain * grad
    inner = jnp.mean(lifted * unit, axis=-1, keepdims=True)
    grad_rows = inverse * (lifted - jnp.mean(lifted, axis=-1, keepdims=True) - unit * inner)
    return grad_rows, jnp.sum(grad * unit, axis=0)


def solution(mesh):
    n_row = mesh.shape["row"]
    n_col = mesh.shape["col"]
    row_bits = n_row.bit_length() - 1
    col_bits = n_col.bit_length() - 1

    def twin(r, c):
        return (r & ~1) | ((c >> 1) & 1), (c & ~2) | ((r & 1) << 1)

    everyone = [(r, c) for r in range(n_row) for c in range(n_col)]

    def permute(value, target):
        pairs = []
        for r, c in everyone:
            to_r, to_c = target(r, c)
            pairs.append((r * n_col + c, to_r * n_col + to_c))
        return lax.ppermute(value, ("row", "col"), pairs)

    def swap(value):
        return permute(value, twin)

    def physical(row_mask, col_mask):
        flip_r = (row_mask & ~1) | ((col_mask >> 1) & 1)
        flip_c = (col_mask & ~2) | ((row_mask & 1) << 1)
        return flip_r, flip_c

    def hop(value, row_mask=0, col_mask=0):
        flip_r, flip_c = physical(row_mask, col_mask)
        return permute(value, lambda r, c: (r ^ flip_r, c ^ flip_c))

    scatter_bits = [1] + list(range(2, col_bits)) + [0]
    gather_bits = scatter_bits[::-1]
    order = [m for m in range(n_col) if not m & 1] + [m for m in range(n_col) if m & 1]

    def gather_col(value):
        parts = {0: value}
        for bit in gather_bits:
            for m in list(parts):
                parts[m | (1 << bit)] = hop(parts[m], col_mask=1 << bit)
        return [parts[m] for m in range(n_col)]

    def gather_row(value):
        parts = {0: value}
        for bit in range(row_bits - 1, -1, -1):
            for m in list(parts):
                parts[m | (1 << bit)] = hop(parts[m], row_mask=1 << bit)
        return [parts[m] for m in range(n_row)]

    def scatter_col(parts):
        parts = dict(enumerate(parts))
        for bit in scatter_bits:
            for m in sorted(parts):
                if not m & (1 << bit):
                    far = hop(parts.pop(m | (1 << bit)).astype(BF), col_mask=1 << bit)
                    parts[m] = parts[m].astype(F32) + far.astype(F32)
        return parts[0]

    def scatter_row(value, me):
        high, wide = value.shape[0] // n_row, value.shape[1]
        held = value.reshape(n_row, high, wide)
        for bit in range(row_bits):
            mine = (me >> bit) & 1
            pairs = held.reshape(held.shape[0] // 2, 2, high, wide)
            send = lax.dynamic_index_in_dim(pairs, 1 - mine, 1, keepdims=False)
            keep = lax.dynamic_index_in_dim(pairs, mine, 1, keepdims=False)
            far = hop(send.astype(BF), row_mask=1 << bit)
            held = keep.astype(F32) + far.astype(F32)
        return swap(held[0].astype(BF)).astype(F32)

    def exchange_cols(value, me, width):
        outs = []
        for m in range(n_col):
            slab = lax.dynamic_slice_in_dim(value, (me ^ m) * width, width, 1)
            outs.append(slab if m == 0 else hop(slab, col_mask=m))
        return outs

    def on_device(
        tokens,
        memory,
        old_memory,
        doc_ids,
        norm_gains,
        comp_weight,
        query_weight,
        key_weight,
        value_weight,
        proj_weight,
        up_weight,
        down_weight,
        cotangent,
    ):
        at_row, at_col = lax.axis_index("row"), lax.axis_index("col")
        me_row, me = twin(at_row, at_col)
        seq, slab = tokens.shape
        mem = memory.shape[0]
        comp = old_memory.shape[0] // RATE
        width = slab * n_col
        seq_b, mem_b, comp_b = seq // n_col, mem // n_col, comp // n_col
        block = comp_b + mem_b + seq_b

        old_rows_own = swap(old_memory).reshape(comp, RATE * slab)
        comp_piece = swap(comp_weight)
        token_piece = swap(tokens)
        memory_piece = swap(memory)
        qkv_piece = swap(jnp.concatenate([query_weight, key_weight, value_weight], axis=1))
        proj_piece = swap(proj_weight.T)
        up_piece = swap(up_weight)
        down_piece = swap(down_weight.T)
        cot_piece = swap(cotangent)
        doc_row = swap(doc_ids)[0]
        gains = lax.dynamic_update_slice_in_dim(
            jnp.zeros((2, width), BF), norm_gains, at_row * norm_gains.shape[1], 1
        )
        for bit in range(row_bits):
            gains = gains + permute(gains, lambda r, c, bit=bit: (r ^ (1 << bit), c))
        gains = gains.astype(F32)
        gain_one, gain_two = gains[0], gains[1]

        old_parts = gather_col(old_rows_own)
        comp_full = stack_rows(gather_row(comp_piece), me_row)
        tile_c = min(comp, 256)
        old_full = assemble(
            old_parts, me, tile_c, comp // tile_c, lambda i, s: i, lambda i: i, comp, taps=RATE
        )
        compressed = nn(old_full, comp_full)

        token_parts = gather_col(token_piece)
        memory_parts = gather_col(memory_piece)
        comp_parts = gather_col(compressed)
        tile = min(seq_b, comp_b + mem_b)
        per = seq_b // tile

        def member(position):
            mask = jnp.int32(order[-1])
            for k in range(n_col - 1):
                mask = jnp.where(position == k, order[k], mask)
            return mask

        blocks = block // comp_b
        normed = assemble(
            memory_parts,
            me,
            mem_b,
            n_col,
            lambda i, s: member(i) ^ s,
            lambda i: i * (block // mem_b) + comp_b // mem_b,
            n_col * block,
            gain=gain_one,
        )
        normed = assemble(
            token_parts,
            me,
            tile,
            n_col * per,
            lambda i, s: (member(i // per) ^ s) * per + i % per,
            lambda i: (i // per) * (block // tile) + (comp_b + mem_b) // tile + i % per,
            n_col * block,
            gain=gain_one,
            base=normed,
        )
        normed = assemble(
            comp_parts,
            me,
            comp_b,
            n_col,
            lambda i, s: member(i) ^ s,
            lambda i: i * blocks,
            n_col * block,
            gain=gain_one,
            base=normed,
        )
        own = lambda parts, high: assemble(parts, me, high, 1, lambda i, s: s, lambda i: i, high)
        own_tokens = own(token_parts, seq_b).astype(F32)
        own_stacked = jnp.concatenate(
            [own(comp_parts, comp_b).astype(F32), own(memory_parts, mem_b).astype(F32), own_tokens], axis=0
        )

        def arranged(natural, high):
            return jnp.stack(
                [lax.dynamic_slice_in_dim(natural, (m ^ me) * high, high) for m in order]
            )

        start = comp + mem
        natural_doc = jnp.concatenate(
            [doc_row[: RATE * comp].reshape(comp, RATE)[:, RATE - 1], doc_row[RATE * comp :]]
        )
        places = jnp.arange(start + seq, dtype=jnp.int32) - start
        reach = (
            jnp.sum((natural_doc[None, :] < natural_doc[start:, None]).astype(jnp.int32), axis=1) - start
        )
        key_place = jnp.concatenate(
            [
                arranged(places[:comp], comp_b),
                arranged(places[comp:start], mem_b),
                arranged(places[start:], seq_b),
            ],
            axis=1,
        ).reshape(-1)
        query_first = arranged(reach, seq_b).reshape(-1)
        query_last = arranged(places[start:], seq_b).reshape(-1)
        q_tiles = seq // tile
        k_tiles = key_place.reshape(-1, tile)
        live = (
            (jnp.max(k_tiles, axis=1)[None, :] >= jnp.min(query_first.reshape(-1, tile), axis=1)[:, None])
            & (jnp.min(k_tiles, axis=1)[None, :] <= jnp.max(query_last.reshape(-1, tile), axis=1)[:, None])
        ).astype(jnp.int32).reshape(-1)
        query_rows = jnp.stack([query_first, query_last])
        key_column = key_place[:, None]

        qkv_full = stack_rows(gather_row(qkv_piece), me_row)
        qkv = nn(normed, qkv_full)
        attend_half = functools.partial(
            attend, qkv, live, query_rows, key_column, slab, tile, per, q_tiles // 2
        )
        mixed_b, level_b = attend_half(q_tiles // 2)
        mixed_a, level_a = attend_half(0)
        proj_full = stack_rows(gather_row(proj_piece), me_row)
        half = n_col // 2

        def by_mask(low, high):
            parts = [None] * n_col
            for k in range(half):
                parts[order[k]] = low[k * (low.shape[0] // half) : (k + 1) * (low.shape[0] // half)]
                parts[order[half + k]] = high[
                    k * (high.shape[0] // half) : (k + 1) * (high.shape[0] // half)
                ]
            return parts

        branch_b = nt(mixed_b, proj_full)
        branch_a = nt(mixed_a, proj_full)
        resid = own_tokens + scatter_col(by_mask(branch_a, branch_b))
        unit_two, _ = statistics(resid)
        hidden_own = (unit_two * gain_two).astype(BF)
        hidden_parts = gather_col(hidden_own)
        hidden_a = jnp.concatenate([hidden_parts[m] for m in order[:half]], axis=0)
        hidden_b = jnp.concatenate([hidden_parts[m] for m in order[half:]], axis=0)

        up_full = stack_rows(gather_row(up_piece), me_row)
        down_full = stack_rows(gather_row(down_piece), me_row)
        cot_parts = gather_col(cot_piece)
        cot_full = assemble(
            cot_parts,
            me,
            tile,
            n_col * per,
            lambda i, s: (member(i // per) ^ s) * per + i % per,
            lambda i: i,
            seq,
        )
        cot_a, cot_b = cot_full[: seq // 2], cot_full[seq // 2 :]
        cot_own = cot_full[:seq_b]

        def feed(hidden, cot):
            upper = nn(hidden, up_full, F32)
            active, pull = jax.vjp(jax.nn.gelu, upper)
            active = active.astype(BF)
            grad_active = nn(cot, down_full, F32)
            grad_upper = pull(grad_active)[0].astype(BF)
            return active, grad_upper, nt(active, down_full), nt(grad_upper, up_full)

        active_a, gupper_a, down_a, ghidden_a = feed(hidden_a, cot_a)
        active_b, gupper_b, down_b, ghidden_b = feed(hidden_b, cot_b)
        grad_hidden = scatter_col(by_mask(ghidden_a, ghidden_b))
        grad_rows, gain_grad_two = norm_back(resid, gain_two, grad_hidden)
        grad_resid = cot_own.astype(F32) + grad_rows
        branch_grad_parts = gather_col(grad_resid.astype(BF))
        gbranch_a = jnp.concatenate([branch_grad_parts[m] for m in order[:half]], axis=0)
        gbranch_b = jnp.concatenate([branch_grad_parts[m] for m in order[half:]], axis=0)
        final = resid + scatter_col(by_mask(down_a, down_b))
        out_parts = exchange_cols(final.astype(BF), me, slab)
        layer_out = stack_rows([swap(v) for v in out_parts], at_col)

        grad_down = (tn(cot_a, active_a, F32) + tn(cot_b, active_b, F32)).astype(BF)
        grad_up = (tn(hidden_a, gupper_a, F32) + tn(hidden_b, gupper_b, F32)).astype(BF)
        down_part = scatter_row(grad_down, me_row).T
        up_part = scatter_row(grad_up, me_row)

        gmixed_a = nn(gbranch_a, proj_full)
        gmixed_b = nn(gbranch_b, proj_full)
        grad_proj = (tn(gbranch_a, mixed_a, F32) + tn(gbranch_b, mixed_b, F32)).astype(BF)
        proj_part = scatter_row(grad_proj, me_row).T
        gqkv = attend_back(
            qkv,
            live,
            query_rows,
            jnp.concatenate([level_a, level_b], axis=1),
            key_column,
            jnp.concatenate([mixed_a, mixed_b], axis=0),
            jnp.concatenate([gmixed_a, gmixed_b], axis=0),
            slab,
            tile,
            per,
        )
        split = half * block
        back_b = nt(gqkv[split:], qkv_full)
        back_a = nt(gqkv[:split], qkv_full)
        grad_normed = scatter_col(by_mask(back_a, back_b))
        grad_qkv = tn(normed, gqkv)
        qkv_part = scatter_row(grad_qkv, me_row)

        grad_stacked, gain_grad_one = norm_back(own_stacked, gain_one, grad_normed)
        grad_x_own = grad_resid + grad_stacked[comp_b + mem_b :]
        x_parts = exchange_cols(grad_x_own.astype(BF), me, slab)
        grad_x = stack_rows([swap(v) for v in x_parts], at_col, F32)
        gcomp_parts = exchange_cols(grad_stacked[:comp_b].astype(BF), me, slab)
        gcomp = stack_rows(gcomp_parts, me)
        comp_part = scatter_row(tn(old_full, gcomp), me_row)

        gain_grads = jnp.stack([gain_grad_one, gain_grad_two])
        for bit in range(row_bits):
            gain_grads = gain_grads + hop(gain_grads, row_mask=1 << bit)
        for bit in range(col_bits):
            gain_grads = gain_grads + hop(gain_grads, col_mask=1 << bit)
        gains_part = lax.dynamic_slice_in_dim(
            gain_grads, at_row * norm_gains.shape[1], norm_gains.shape[1], 1
        )
        return (
            layer_out,
            grad_x,
            gains_part,
            comp_part,
            qkv_part[:, :slab],
            qkv_part[:, slab : 2 * slab],
            qkv_part[:, 2 * slab :],
            proj_part,
            up_part,
            down_part,
        )

    both, wide, tall = P("row", "col"), P(None, "row"), P("col", "row")
    in_specs = (
        both, both, both, P("row", None), wide, both, both, both, both, tall, both, tall, both,
    )
    out_specs = (both, both, wide, both, both, both, both, tall, both, tall)
    return jax.shard_map(on_device, mesh=mesh, in_specs=in_specs, out_specs=out_specs, check_vma=False)
```
